32 devices in a mesh: occ: 4 (over y, x), vir: 2 (over core), rep: 4 (over z).
Axes of the slice: x: 2, y: 2, z: 4, core: 2. Of those that a mesh axis runs over, the one named last changes fastest.
Arguments:
- integrals: float32 [128, 62500], P('vir', 'rep'), may hold values from -0.0625 to 0.0625
- amplitudes: float32 [62500, 1024], P('rep', ('occ', 'vir')), may hold values from -6 to 6
- vir_irrep: int32 [250], replicated, may hold values from 0 to 7
- occ_irrep: int32 [100], replicated, may hold values from 0 to 7
Outputs:
- ladder: float32 [128, 1024], P('vir', ('occ', 'rep'))
The draws below stay inside these ranges and needn't reach their ends.
Inputs may be any that keep to these rules, and one draw needn't show every extreme that they name: `vir_irrep`: labels of the eight irreps of D2h, combined by XOR. `occ_irrep`: labels of the eight irreps of D2h, combined by XOR.
All inputs are finite; a program needn't handle non-finite values.
Results may differ from the reference program's by a relative error of at most 0.0003.
Values sent between devices are 32-bit elements; how exact they have to be, the bound alone decides.
No kernel may reach another device: no remote copies, remote signals or barrier semaphores. Data moves between devices by JAX's collectives and lax.ppermute only.
A program may use at most 64 MiB of HBM per device.

```python
import jax
import jax.numpy as jnp
from jax import lax

NV = 250
NO = 100
AB_DEV = 64
AB = 128
EF = 62500
IJ = 1024
N_VIR = 2


def place_ends(drawn, rng, least, high):
    place = [jax.random.randint(jax.random.fold_in(rng, axis), (), 0, length) for axis, length in enumerate(drawn.shape)]
    widest = drawn.shape.index(max(drawn.shape))
    neighbour = place[:widest] + [(place[widest] + 1) % drawn.shape[widest]] + place[widest + 1:]
    return drawn.at[tuple(place)].set(least).at[tuple(neighbour)].set(high)


def block_scale(own_key, dims, pieces, least, top_value):
    loudness, own = 1.0, jax.random.fold_in(own_key, 6)
    for position, shards_of in pieces:
        draws = jnp.exp(jax.random.uniform(jax.random.fold_in(own, position), (shards_of,), jnp.float32, least / len(pieces), top_value / len(pieces)))
        loudness = loudness * jnp.repeat(draws, dims[position] // shards_of).reshape([-1 if axis == position else 1 for axis in range(len(dims))])
    return loudness


def centred(rng, dims, spread, bound, pieces=(), held_as=jnp.bfloat16):
    loudness = block_scale(rng, dims, pieces, -0.22, 0.18) if pieces else 1.0
    drawn = jax.random.normal(rng, dims, jnp.float32) * spread * loudness
    return jnp.minimum(jnp.maximum(drawn, -bound), bound).astype(held_as)


def setup_inputs(seed: int = 0) -> dict:
    streams_of = jax.random.split(jax.random.key(seed), 5)
    integrals = centred(streams_of[0], (AB, EF), (EF // 8) ** -0.5, 0.0625, ((0, 2), (1, 4)), jnp.float32)
    amplitudes = centred(streams_of[1], (EF, IJ), 1.0, 6.0, ((0, 4), (1, 8)), jnp.float32)
    vir_irrep = place_ends(jax.random.randint(streams_of[2], (NV,), 0, 8), jax.random.fold_in(streams_of[2], 1), 0, 7).astype(jnp.int32)
    occ_irrep = place_ends(jax.random.randint(streams_of[3], (NO,), 0, 8), jax.random.fold_in(streams_of[3], 1), 0, 7).astype(jnp.int32)
    return {"integrals": integrals, "amplitudes": amplitudes, "vir_irrep": vir_irrep, "occ_irrep": occ_irrep}


def pair_labels(table, width, count):
    pairs = jnp.arange(count, dtype=jnp.int32)
    return jnp.bitwise_xor(table[pairs // width], table[pairs % width])


def reference(integrals, amplitudes, vir_irrep, occ_irrep):
    g_ab = pair_labels(vir_irrep, NV, AB)
    g_ef = pair_labels(vir_irrep, NV, EF)
    g_ij = pair_labels(occ_irrep, NO, IJ)
    t_sym = jnp.where(g_ef[:, None] == g_ij[None, :], amplitudes, jnp.float32(0.0))
    blocks = integrals.reshape(N_VIR, AB_DEV, EF)
    labels = g_ab.reshape(N_VIR, AB_DEV)

    def one_block(item):
        rows, row_labels = item
        v_sym = jnp.where(row_labels[:, None] == g_ef[None, :], rows, jnp.float32(0.0))
        return jnp.dot(v_sym, t_sym, precision=lax.Precision.HIGHEST, preferred_element_type=jnp.float32)

    result = lax.map(one_block, (blocks, labels))
    return result.reshape(AB, IJ)
```

```python
import jax
import jax.numpy as jnp
from jax import lax
from jax.experimental import pallas as pl
from jax.experimental.pallas import tpu as pltpu
from jax.sharding import PartitionSpec as P

LANES = 128
KB = 2048


def lookup(table_ref, ids):
    found = None
    low = jnp.bitwise_and(ids, LANES - 1)
    for part in range(table_ref.shape[1] // LANES):
        row = jnp.broadcast_to(table_ref[:, part * LANES:(part + 1) * LANES], ids.shape)
        here = jnp.take_along_axis(row, low, axis=1, mode="promise_in_bounds")
        found = here if found is None else jnp.where(ids >= part * LANES, here, found)
    return found


def pair_labels(table_ref, width, ids):
    first = lax.div(ids, jnp.int32(width))
    return jnp.bitwise_xor(lookup(table_ref, first), lookup(table_ref, ids - first * width))


def halves(x):
    high = x.astype(jnp.bfloat16)
    return high, (x - high.astype(jnp.float32)).astype(jnp.bfloat16)


def masked_product(v, t, vir_irrep, occ_irrep, ab_from_partner, n_vir, gathered=False):
    rows, depth = v.shape
    cols = t.shape[1]
    nv, no = vir_irrep.shape[0], occ_irrep.shape[0]
    steps = pl.cdiv(depth, KB)
    tail = depth - (steps - 1) * KB
    vpad = pl.cdiv(nv, LANES) * LANES
    opad = pl.cdiv(no, LANES) * LANES

    def kernel(vtab, otab, v_ref, t_ref, out_ref, gab, vs, ts, acc):
        step = pl.program_id(0)
        vir = lax.axis_index("vir")
        block = (n_vir - 1 - vir) if ab_from_partner else vir

        @pl.when(step == 0)
        def _():
            ids = block * rows + lax.broadcasted_iota(jnp.int32, (rows, LANES), 0)
            gab[...] = pair_labels(vtab, nv, ids)
            acc[...] = jnp.zeros_like(acc)

        sub = KB // LANES
        local = step * KB + (lax.broadcasted_iota(jnp.int32, (sub, LANES), 0) * LANES
                             + lax.broadcasted_iota(jnp.int32, (sub, LANES), 1))
        g_ef = pair_labels(vtab, nv, lax.axis_index("rep") * depth + local)
        g_ef = jnp.where(local < depth, g_ef, -1)
        labels = gab[...]
        for j in range(sub):
            keep = labels == g_ef[j:j + 1, :]
            high, low = halves(jnp.where(keep, v_ref[:, j * LANES:(j + 1) * LANES], 0.0))
            vs[:rows, j * LANES:(j + 1) * LANES] = high
            vs[rows:, j * LANES:(j + 1) * LANES] = low
        high, low = halves(t_ref[...])
        ts[:, :cols] = high
        ts[:, cols:] = low
        if tail < KB:
            base = tail // 16 * 16

            @pl.when(step == steps - 1)
            def _():
                at = base + lax.broadcasted_iota(jnp.int32, (KB - base, 2 * cols), 0)
                ts[base:, :] = jnp.where(at < tail, ts[base:, :].astype(jnp.float32), 0.0).astype(jnp.bfloat16)

        acc[...] += jnp.dot(vs[...], ts[...], preferred_element_type=jnp.float32)

        @pl.when(step == steps - 1)
        def _():
            total = (acc[:rows, :cols] + (acc[:rows, cols:] + acc[rows:, :cols])) + acc[rows:, cols:]
            occ = lax.axis_index("occ")
            col0 = (occ if gathered else occ * n_vir + vir) * cols
            for j in range(cols // LANES):
                ids = col0 + j * LANES + lax.broadcasted_iota(jnp.int32, (8, LANES), 1)
                g_ij = pair_labels(otab, no, ids)[0:1, :]
                part = total[:, j * LANES:(j + 1) * LANES]
                out_ref[:, j * LANES:(j + 1) * LANES] = jnp.where(labels == g_ij, part, 0.0)

    return pl.pallas_call(
        kernel,
        grid=(steps,),
        in_specs=[
            pl.BlockSpec((1, vpad), lambda k: (0, 0)),
            pl.BlockSpec((1, opad), lambda k: (0, 0)),
            pl.BlockSpec((rows, KB), lambda k: (0, k)),
            pl.BlockSpec((KB, cols), lambda k: (k, 0)),
        ],
        out_specs=pl.BlockSpec((rows, cols), lambda k: (0, 0)),
        out_shape=jax.ShapeDtypeStruct((rows, cols), jnp.float32),
        scratch_shapes=[
            pltpu.VMEM((rows, LANES), jnp.int32),
            pltpu.VMEM((2 * rows, KB), jnp.bfloat16),
            pltpu.VMEM((KB, 2 * cols), jnp.bfloat16),
            pltpu.VMEM((2 * rows, 2 * cols), jnp.float32),
        ],
    )(vir_irrep.reshape(1, nv), occ_irrep.reshape(1, no), v, t)


def per_device(integrals, amplitudes, vir_irrep, occ_irrep):
    n_vir, n_rep = lax.axis_size("vir"), lax.axis_size("rep")
    cols = amplitudes.shape[1]
    if n_vir != 2 or n_rep % 2 or cols % LANES:
        piece = lax.all_gather(amplitudes, "vir", axis=1, tiled=True)
        partial = masked_product(integrals, piece, vir_irrep, occ_irrep, False, n_vir, gathered=True)
        return lax.psum_scatter(partial, "rep", scatter_dimension=1, tiled=True)

    other = lax.ppermute(integrals, "vir", [(0, 1), (1, 0)])
    own_part = masked_product(integrals, amplitudes, vir_irrep, occ_irrep, False, n_vir)
    other_part = masked_product(other, amplitudes, vir_irrep, occ_irrep, True, n_vir)

    per = n_rep // 2
    width = cols // per
    vir, rep = lax.axis_index("vir"), lax.axis_index("rep")
    low = jnp.where(vir == 0, own_part, other_part)
    high = jnp.where(vir == 0, other_part, own_part)
    pieces = jnp.stack([p[:, h * width:(h + 1) * width] for p in (low, high) for h in range(per)])
    total = None
    for k in range(n_rep):
        perm = []
        for w in range(2):
            for r in range(n_rep):
                i = (r + k) % n_rep
                perm.append((w * n_rep + r, (i // per) * n_rep + w * per + i % per))
        mine = lax.dynamic_index_in_dim(pieces, (rep + k) % n_rep, 0, keepdims=False)
        got = lax.ppermute(mine, ("vir", "rep"), perm)
        total = got if total is None else total + got
    return total


def solution(mesh):
    return jax.shard_map(
        per_device,
        mesh=mesh,
        in_specs=(P("vir", "rep"), P("rep", ("occ", "vir")), P(), P()),
        out_specs=P("vir", ("occ", "rep")),
        check_vma=False,
    )
```

```python
import jax
import jax.numpy as jnp
from jax import lax
from jax.experimental import pallas as pl
from jax.experimental.pallas import tpu as pltpu
from jax.sharding import PartitionSpec as P

LANES = 128
SUB = 256
CHUNK = 2048


def lookup(table_ref, ids):
    found = None
    low = jnp.bitwise_and(ids, LANES - 1)
    for part in range(table_ref.shape[1] // LANES):
        row = jnp.broadcast_to(table_ref[:, part * LANES:(part + 1) * LANES], ids.shape)
        here = jnp.take_along_axis(row, low, axis=1, mode="promise_in_bounds")
        found = here if found is None else jnp.where(ids >= part * LANES, here, found)
    return found


def pair_labels(table_ref, width, ids):
    first = lax.div(ids, jnp.int32(width))
    return jnp.bitwise_xor(lookup(table_ref, first), lookup(table_ref, ids - first * width))


def halves(x):
    high = x.astype(jnp.bfloat16)
    return high, (x - high.astype(jnp.float32)).astype(jnp.bfloat16)


def up(size, unit):
    return pl.cdiv(size, unit) * unit


def iota(shape, axis):
    return lax.broadcasted_iota(jnp.int32, shape, axis)


def joined(parts):
    return parts[0] if len(parts) == 1 else jnp.concatenate(parts, axis=1)


def kept_columns(total, labels, otab, no, col0):
    parts = []
    for j in range(total.shape[1] // LANES):
        g_ij = pair_labels(otab, no, col0 + j * LANES + iota((8, LANES), 1))[0:1, :]
        parts.append(jnp.where(labels == g_ij, total[:, j * LANES:(j + 1) * LANES], 0.0))
    return joined(parts)


def padded_table(scratch, table_ref):
    scratch[:, :table_ref.shape[1]] = table_ref[...]


def folded(both, rows, cols):
    return (both[:rows, :cols] + (both[:rows, cols:] + both[rows:, :cols])) + both[rows:, cols:]


def chunks_of(depth):
    return [(at, min(CHUNK, depth - at)) for at in range(0, depth, CHUNK)]


def masked_rows(v_ref, first, g_ref, labels, at, size):
    high, low = [], []
    for j in range(at // LANES, (at + size) // LANES):
        keep = labels == g_ref[j:j + 1, :]
        h, l = halves(jnp.where(keep, v_ref[:, j * LANES - first:(j + 1) * LANES - first], 0.0))
        high.append(h)
        low.append(l)
    return jnp.concatenate([joined(high), joined(low)], axis=0)


def tails_of(v, t):
    base = t.shape[0] // LANES * LANES
    fill = LANES - (t.shape[0] - base)
    return [jnp.pad(v[:, base:], ((0, 0), (0, fill))), jnp.pad(t[base:], ((0, fill), (0, 0)))]


def own_product(v, t, vir_irrep):
    rows, depth = v.shape
    cols = t.shape[1]
    nv = vir_irrep.shape[0]
    base = depth // LANES * LANES
    tiles = up(pl.cdiv(depth, LANES), 8)
    parts = chunks_of(base)

    def kernel(vir_ref, v_hbm, t_hbm, part_ref, high_ref, low_ref, g_ref, raw, vtab, vbuf, tbuf, rsem, vsem, tsem):
        labels_in = pltpu.make_async_copy(vir_ref, raw, rsem)
        labels_in.start()
        copies = []
        for c, (at, size) in enumerate(parts):
            cv = pltpu.make_async_copy(v_hbm.at[:, pl.ds(at, size)], vbuf.at[:, pl.ds(at, size)], vsem.at[c])
            ct = pltpu.make_async_copy(t_hbm.at[pl.ds(at, size), :], tbuf.at[pl.ds(at, size), :], tsem.at[c])
            cv.start()
            ct.start()
            copies.append((cv, ct))
        labels_in.wait()
        padded_table(vtab, raw)
        local = iota((tiles, LANES), 0) * LANES + iota((tiles, LANES), 1)
        g_ef = pair_labels(vtab, nv, lax.axis_index("rep") * depth + local)
        g_ref[...] = jnp.where(local < depth, g_ef, -1)
        labels = pair_labels(vtab, nv, lax.axis_index("vir") * rows + iota((rows, LANES), 0))
        total = None
        for c, (at, size) in enumerate(parts):
            copies[c][0].wait()
            copies[c][1].wait()
            for s in range(at, at + size, SUB):
                end = min(s + SUB, at + size)
                high, low = halves(tbuf[s:end, :])
                high_ref[s:end, :] = high
                low_ref[s:end, :] = low
                got = jnp.dot(masked_rows(vbuf, 0, g_ref, labels, s, end - s), jnp.concatenate([high, low], axis=1),
                              preferred_element_type=jnp.float32)
                total = got if total is None else total + got
        part_ref[...] = folded(total, rows, cols)

    vmem = pl.BlockSpec(memory_space=pltpu.VMEM)
    hbm = pl.BlockSpec(memory_space=pltpu.HBM)
    return pl.pallas_call(
        kernel,
        in_specs=[hbm, hbm, hbm],
        out_specs=[vmem] * 4,
        out_shape=[
            pltpu.VMEM((rows, cols), jnp.float32),
            pltpu.VMEM((base, cols), jnp.bfloat16),
            pltpu.VMEM((base, cols), jnp.bfloat16),
            pltpu.VMEM((tiles, LANES), jnp.int32),
        ],
        scratch_shapes=[
            pltpu.VMEM((1, nv), jnp.int32),
            pltpu.VMEM((1, up(nv, LANES)), jnp.int32),
            pltpu.VMEM((rows, base), jnp.float32),
            pltpu.VMEM((base, cols), jnp.float32),
            pltpu.SemaphoreType.DMA(()),
            pltpu.SemaphoreType.DMA((len(parts),)),
            pltpu.SemaphoreType.DMA((len(parts),)),
        ],
        compiler_params=pltpu.CompilerParams(vmem_limit_bytes=32 << 20),
        name="own",
    )(*(pltpu.with_memory_space_constraint(x, pltpu.HBM) for x in (vir_irrep.reshape(1, nv), v, t)))


def messages(v, tails, part, high, low, g_ef, vir_irrep, occ_irrep):
    rows, depth = v.shape
    cols = high.shape[1]
    width = cols // 2
    nv, no = vir_irrep.shape[0], occ_irrep.shape[0]
    base = depth // LANES * LANES

    def kernel(vir_ref, occ_ref, v_ref, *refs):
        tail_refs = refs[:len(tails)]
        part_ref, high_ref, low_ref, g_ref, out0, out1, vtab, otab, rest = refs[len(tails):]
        vir, rep, occ = lax.axis_index("vir"), lax.axis_index("rep"), lax.axis_index("occ")
        padded_table(vtab, vir_ref)
        padded_table(otab, occ_ref)
        mine = pair_labels(vtab, nv, vir * rows + iota((rows, LANES), 0))
        theirs = pair_labels(vtab, nv, (1 - vir) * rows + iota((rows, LANES), 0))
        total = None
        own = part_ref[...]
        if tails:
            v_tail, t_tail = tail_refs
            both = jnp.concatenate(halves(t_tail[...]), axis=1)
            rest[...] = jnp.zeros_like(rest)
            rest[:, :depth - base] = v_ref[:, base:]
            total = jnp.dot(masked_rows(rest, base, g_ref, theirs, base, LANES), both, preferred_element_type=jnp.float32)
            more = jnp.dot(masked_rows(v_tail, base, g_ref, mine, base, LANES), both, preferred_element_type=jnp.float32)
            own = own + folded(more, rows, cols)
        for s in range(0, base, SUB):
            end = min(s + SUB, base)
            both = jnp.concatenate([high_ref[s:end, :], low_ref[s:end, :]], axis=1)
            got = jnp.dot(masked_rows(v_ref, 0, g_ref, theirs, s, end - s), both, preferred_element_type=jnp.float32)
            total = got if total is None else total + got
        col0 = (occ * 2 + vir) * cols
        own = kept_columns(own, mine, otab, no, col0)
        other = kept_columns(folded(total, rows, cols), theirs, otab, no, col0)
        same = vir == lax.div(rep, 2)
        first = jnp.where(same, other, own)
        second = jnp.where(same, own, other)
        upper = jnp.logical_xor(lax.rem(rep, 2) == 1, same)
        first_turned = pltpu.roll(first, width, 1)
        second_turned = pltpu.roll(second, width, 1)
        left = iota((rows, cols), 1) < width
        out0[...] = jnp.where(left, jnp.where(upper, first_turned, first), jnp.where(upper, second, second_turned))
        out1[...] = jnp.where(left, jnp.where(upper, first, first_turned), jnp.where(upper, second_turned, second))

    vmem = pl.BlockSpec(memory_space=pltpu.VMEM)
    return pl.pallas_call(
        kernel,
        in_specs=[vmem] * (7 + len(tails)),
        out_specs=[vmem] * 2,
        out_shape=[jax.ShapeDtypeStruct((rows, cols), jnp.float32)] * 2,
        scratch_shapes=[
            pltpu.VMEM((1, up(nv, LANES)), jnp.int32),
            pltpu.VMEM((1, up(no, LANES)), jnp.int32),
            pltpu.VMEM((rows, LANES), jnp.float32),
        ],
        compiler_params=pltpu.CompilerParams(vmem_limit_bytes=32 << 20),
        name="messages",
    )(vir_irrep.reshape(1, nv), occ_irrep.reshape(1, no), v, *tails, part, high, low, g_ef)


def gathered_product(v, t, vir_irrep, occ_irrep):
    rows, depth = v.shape
    cols = t.shape[1]
    nv, no = vir_irrep.shape[0], occ_irrep.shape[0]
    steps = pl.cdiv(depth, CHUNK)

    def kernel(vtab, otab, v_ref, t_ref, out_ref, g_ref, acc):
        step = pl.program_id(0)
        labels = pair_labels(vtab, nv, lax.axis_index("vir") * rows + iota((rows, LANES), 0))
        shape = (CHUNK // LANES, LANES)
        local = step * CHUNK + iota(shape, 0) * LANES + iota(shape, 1)
        g_ef = pair_labels(vtab, nv, lax.axis_index("rep") * depth + local)
        g_ref[...] = jnp.where(local < depth, g_ef, -1)
        total = None
        for s in range(0, CHUNK, SUB):
            block = jnp.where(step * CHUNK + s + iota((SUB, cols), 0) < depth, t_ref[s:s + SUB, :], 0.0)
            both = jnp.concatenate(halves(block), axis=1)
            got = jnp.dot(masked_rows(v_ref, 0, g_ref, labels, s, SUB), both, preferred_element_type=jnp.float32)
            total = got if total is None else total + got
        acc[...] = jnp.where(step == 0, total, acc[...] + total)

        @pl.when(step == steps - 1)
        def _():
            out_ref[...] = kept_columns(folded(acc[...], rows, cols), labels, otab, no, lax.axis_index("occ") * cols)

    return pl.pallas_call(
        kernel,
        grid=(steps,),
        in_specs=[
            pl.BlockSpec((1, up(nv, LANES)), lambda k: (0, 0)),
            pl.BlockSpec((1, up(no, LANES)), lambda k: (0, 0)),
            pl.BlockSpec((rows, CHUNK), lambda k: (0, k)),
            pl.BlockSpec((CHUNK, cols), lambda k: (k, 0)),
        ],
        out_specs=pl.BlockSpec((rows, cols), lambda k: (0, 0)),
        out_shape=jax.ShapeDtypeStruct((rows, cols), jnp.float32),
        scratch_shapes=[
            pltpu.VMEM((CHUNK // LANES, LANES), jnp.int32),
            pltpu.VMEM((2 * rows, 2 * cols), jnp.float32),
        ],
        name="gathered",
    )(vir_irrep.reshape(1, nv), occ_irrep.reshape(1, no), v, t)


def reduced(first, second):
    to_first, to_second = [], []
    for z in range(4):
        b = z // 2
        to_first += [(b * 4 + z, (1 - (z ^ 1) // 2) * 4 + (z ^ 1)), ((1 - b) * 4 + z, ((z ^ 2) // 2) * 4 + (z ^ 2))]
        to_second += [(b * 4 + z, (1 - b) * 4 + z), ((1 - b) * 4 + z, ((z ^ 3) // 2) * 4 + (z ^ 3))]
    got = lax.ppermute(first, ("vir", "rep"), to_first) + lax.ppermute(second, ("vir", "rep"), to_second)
    width = got.shape[1] // 2
    return got[:, :width] + lax.ppermute(got[:, width:], "vir", [(0, 1), (1, 0)])


def per_device(integrals, amplitudes, vir_irrep, occ_irrep):
    rows, depth = integrals.shape
    cols = amplitudes.shape[1]
    if lax.axis_size("vir") != 2 or lax.axis_size("rep") != 4 or cols != LANES or rows % 16:
        piece = lax.all_gather(amplitudes, "vir", axis=1, tiled=True)
        partial = gathered_product(integrals, piece, vir_irrep, occ_irrep)
        return lax.psum_scatter(partial, "rep", scatter_dimension=1, tiled=True)

    other = lax.ppermute(integrals, "vir", [(0, 1), (1, 0)])
    part, high, low, g_ef = own_product(integrals, amplitudes, vir_irrep)
    tails = []
    if depth % LANES:
        v, t, part = lax.optimization_barrier((integrals, amplitudes, part))
        tails = tails_of(v, t)
    first, second = messages(other, tails, part, high, low, g_ef, vir_irrep, occ_irrep)
    return reduced(first, second)


def solution(mesh):
    return jax.shard_map(
        per_device,
        mesh=mesh,
        in_specs=(P("vir", "rep"), P("rep", ("occ", "vir")), P(), P()),
        out_specs=P("vir", ("occ", "rep")),
        check_vma=False,
    )
```

```python
import jax
import jax.numpy as jnp
from jax import lax
from jax.experimental import pallas as pl
from jax.experimental.pallas import tpu as pltpu
from jax.sharding import PartitionSpec as P

LANES = 128
SUB = 256
CHUNK = 2048
GROUP = 16


def lookup(table_ref, ids):
    found = None
    low = jnp.bitwise_and(ids, LANES - 1)
    for part in range(table_ref.shape[1] // LANES):
        row = jnp.broadcast_to(table_ref[:, part * LANES:(part + 1) * LANES], ids.shape)
        here = jnp.take_along_axis(row, low, axis=1, mode="promise_in_bounds")
        found = here if found is None else jnp.where(ids >= part * LANES, here, found)
    return found


def pair_labels(table_ref, width, ids):
    first = lax.div(ids, jnp.int32(width))
    return jnp.bitwise_xor(lookup(table_ref, first), lookup(table_ref, ids - first * width))


def halves(x):
    high = x.astype(jnp.bfloat16)
    return high, (x - high.astype(jnp.float32)).astype(jnp.bfloat16)


def up(size, unit):
    return pl.cdiv(size, unit) * unit


def iota(shape, axis):
    return lax.broadcasted_iota(jnp.int32, shape, axis)


def joined(parts):
    return parts[0] if len(parts) == 1 else jnp.concatenate(parts, axis=1)


def kept_columns(total, labels, otab, no, col0):
    parts = []
    for j in range(total.shape[1] // LANES):
        g_ij = pair_labels(otab, no, col0 + j * LANES + iota((8, LANES), 1))[0:1, :]
        parts.append(jnp.where(labels == g_ij, total[:, j * LANES:(j + 1) * LANES], 0.0))
    return joined(parts)


def padded_table(scratch, table_ref):
    scratch[:, :table_ref.shape[1]] = table_ref[...]


def folded(both, rows, cols):
    return (both[:rows, :cols] + (both[:rows, cols:] + both[rows:, :cols])) + both[rows:, cols:]


def chunks_of(depth):
    return [(at, min(CHUNK, depth - at)) for at in range(0, depth, CHUNK)]


def masked_rows(v_ref, first, g_ref, labels, at, size):
    high, low = [], []
    for j in range(at // LANES, (at + size) // LANES):
        keep = labels == g_ref[j:j + 1, :]
        h, l = halves(jnp.where(keep, v_ref[:, j * LANES - first:(j + 1) * LANES - first], 0.0))
        high.append(h)
        low.append(l)
    return jnp.concatenate([joined(high), joined(low)], axis=0)


def tails_of(v, t):
    base = t.shape[0] // LANES * LANES
    fill = LANES - (t.shape[0] - base)
    return [v, jnp.pad(t[base:], ((0, fill), (0, 0)))]


def own_product(v, t, vir_irrep):
    rows, depth = v.shape
    cols = t.shape[1]
    nv = vir_irrep.shape[0]
    base = depth // LANES * LANES
    tiles = up(pl.cdiv(depth, LANES), 8)
    parts = chunks_of(base)
    tail = int(depth > base)

    def kernel(vir_ref, v_hbm, t_hbm, *refs):
        part_ref, high_ref, low_ref, g_ref = refs[:4]
        raw, vtab, vbuf, tbuf, rsem, vsem, tsem = refs[-7:]
        labels_in = pltpu.make_async_copy(vir_ref, raw, rsem)
        labels_in.start()
        rows_in = [pltpu.make_async_copy(v_hbm.at[pl.ds(i * GROUP, GROUP), :], vbuf.at[pl.ds(i * GROUP, GROUP), :], vsem.at[i])
                   for i in range(rows // GROUP)]
        parts_in = [pltpu.make_async_copy(t_hbm.at[pl.ds(at, size), :], tbuf.at[pl.ds(at, size), :], tsem.at[c])
                    for c, (at, size) in enumerate(parts)]
        for copy in rows_in + parts_in:
            copy.start()
        labels_in.wait()
        padded_table(vtab, raw)
        local = iota((tiles, LANES), 0) * LANES + iota((tiles, LANES), 1)
        g_ef = pair_labels(vtab, nv, lax.axis_index("rep") * depth + local)
        g_ref[...] = jnp.where(local < depth, g_ef, -1)
        labels = pair_labels(vtab, nv, lax.axis_index("vir") * rows + iota((rows, LANES), 0))
        for copy in rows_in:
            copy.wait()
        if depth > base:
            rest = refs[4]
            rest[...] = jnp.zeros_like(rest)
            rest[:, :depth - base] = vbuf[:, base:]
        total = None
        for c, (at, size) in enumerate(parts):
            parts_in[c].wait()
            for s in range(at, at + size, SUB):
                end = min(s + SUB, at + size)
                high, low = halves(tbuf[s:end, :])
                high_ref[s:end, :] = high
                low_ref[s:end, :] = low
                got = jnp.dot(masked_rows(vbuf, 0, g_ref, labels, s, end - s), jnp.concatenate([high, low], axis=1),
                              preferred_element_type=jnp.float32)
                total = got if total is None else total + got
        part_ref[...] = folded(total, rows, cols)

    vmem = pl.BlockSpec(memory_space=pltpu.VMEM)
    hbm = pl.BlockSpec(memory_space=pltpu.HBM)
    return pl.pallas_call(
        kernel,
        in_specs=[hbm, hbm, hbm],
        out_specs=[vmem] * (4 + tail),
        out_shape=[
            pltpu.VMEM((rows, cols), jnp.float32),
            pltpu.VMEM((base, cols), jnp.bfloat16),
            pltpu.VMEM((base, cols), jnp.bfloat16),
            pltpu.VMEM((tiles, LANES), jnp.int32),
        ] + [pltpu.VMEM((rows, LANES), jnp.float32)] * tail,
        scratch_shapes=[
            pltpu.VMEM((1, nv), jnp.int32),
            pltpu.VMEM((1, up(nv, LANES)), jnp.int32),
            pltpu.VMEM((rows, depth), jnp.float32),
            pltpu.VMEM((base, cols), jnp.float32),
            pltpu.SemaphoreType.DMA(()),
            pltpu.SemaphoreType.DMA((rows // GROUP,)),
            pltpu.SemaphoreType.DMA((len(parts),)),
        ],
        compiler_params=pltpu.CompilerParams(vmem_limit_bytes=32 << 20),
        name="own",
    )(*(pltpu.with_memory_space_constraint(x, pltpu.HBM) for x in (vir_irrep.reshape(1, nv), v, t)))


def messages(v, tails, part, high, low, g_ef, vir_irrep, occ_irrep):
    rows, depth = v.shape
    cols = high.shape[1]
    width = cols // 2
    nv, no = vir_irrep.shape[0], occ_irrep.shape[0]
    base = depth // LANES * LANES

    def kernel(vir_ref, occ_ref, v_ref, *refs):
        tail_refs = refs[:len(tails)]
        part_ref, high_ref, low_ref, g_ref, out0, out1, vtab, otab, rest = refs[len(tails):]
        vir, rep, occ = lax.axis_index("vir"), lax.axis_index("rep"), lax.axis_index("occ")
        padded_table(vtab, vir_ref)
        padded_table(otab, occ_ref)
        mine = pair_labels(vtab, nv, vir * rows + iota((rows, LANES), 0))
        theirs = pair_labels(vtab, nv, (1 - vir) * rows + iota((rows, LANES), 0))
        total = None
        own = part_ref[...]
        if tails:
            v_tail, t_tail = tail_refs
            both = jnp.concatenate(halves(t_tail[...]), axis=1)
            rest[...] = jnp.zeros_like(rest)
            rest[:, :depth - base] = v_ref[:, base:]
            total = jnp.dot(masked_rows(rest, base, g_ref, theirs, base, LANES), both, preferred_element_type=jnp.float32)
            more = jnp.dot(masked_rows(v_tail, base, g_ref, mine, base, LANES), both, preferred_element_type=jnp.float32)
            own = own + folded(more, rows, cols)
        for s in range(0, base, SUB):
            end = min(s + SUB, base)
            both = jnp.concatenate([high_ref[s:end, :], low_ref[s:end, :]], axis=1)
            got = jnp.dot(masked_rows(v_ref, 0, g_ref, theirs, s, end - s), both, preferred_element_type=jnp.float32)
            total = got if total is None else total + got
        col0 = (occ * 2 + vir) * cols
        own = kept_columns(own, mine, otab, no, col0)
        other = kept_columns(folded(total, rows, cols), theirs, otab, no, col0)
        same = vir == lax.div(rep, 2)
        first = jnp.where(same, other, own)
        second = jnp.where(same, own, other)
        upper = lax.rem(rep, 2) == 0
        first_turned = pltpu.roll(first, width, 1)
        second_turned = pltpu.roll(second, width, 1)
        left = iota((rows, cols), 1) < width
        out0[...] = jnp.where(left, jnp.where(upper, first_turned, first), jnp.where(upper, second, second_turned))
        out1[...] = jnp.where(left, jnp.where(upper, first, first_turned), jnp.where(upper, second_turned, second))

    vmem = pl.BlockSpec(memory_space=pltpu.VMEM)
    return pl.pallas_call(
        kernel,
        in_specs=[vmem] * (7 + len(tails)),
        out_specs=[vmem] * 2,
        out_shape=[jax.ShapeDtypeStruct((rows, cols), jnp.float32)] * 2,
        scratch_shapes=[
            pltpu.VMEM((1, up(nv, LANES)), jnp.int32),
            pltpu.VMEM((1, up(no, LANES)), jnp.int32),
            pltpu.VMEM((rows, LANES), jnp.float32),
        ],
        compiler_params=pltpu.CompilerParams(vmem_limit_bytes=32 << 20),
        name="messages",
    )(vir_irrep.reshape(1, nv), occ_irrep.reshape(1, no), v, *tails, part, high, low, g_ef)


def gathered_product(v, t, vir_irrep, occ_irrep):
    rows, depth = v.shape
    cols = t.shape[1]
    nv, no = vir_irrep.shape[0], occ_irrep.shape[0]
    steps = pl.cdiv(depth, CHUNK)

    def kernel(vtab, otab, v_ref, t_ref, out_ref, g_ref, acc):
        step = pl.program_id(0)
        labels = pair_labels(vtab, nv, lax.axis_index("vir") * rows + iota((rows, LANES), 0))
        shape = (CHUNK // LANES, LANES)
        local = step * CHUNK + iota(shape, 0) * LANES + iota(shape, 1)
        g_ef = pair_labels(vtab, nv, lax.axis_index("rep") * depth + local)
        g_ref[...] = jnp.where(local < depth, g_ef, -1)
        total = None
        for s in range(0, CHUNK, SUB):
            block = jnp.where(step * CHUNK + s + iota((SUB, cols), 0) < depth, t_ref[s:s + SUB, :], 0.0)
            both = jnp.concatenate(halves(block), axis=1)
            got = jnp.dot(masked_rows(v_ref, 0, g_ref, labels, s, SUB), both, preferred_element_type=jnp.float32)
            total = got if total is None else total + got
        acc[...] = jnp.where(step == 0, total, acc[...] + total)

        @pl.when(step == steps - 1)
        def _():
            out_ref[...] = kept_columns(folded(acc[...], rows, cols), labels, otab, no, lax.axis_index("occ") * cols)

    return pl.pallas_call(
        kernel,
        grid=(steps,),
        in_specs=[
            pl.BlockSpec((1, up(nv, LANES)), lambda k: (0, 0)),
            pl.BlockSpec((1, up(no, LANES)), lambda k: (0, 0)),
            pl.BlockSpec((rows, CHUNK), lambda k: (0, k)),
            pl.BlockSpec((CHUNK, cols), lambda k: (k, 0)),
        ],
        out_specs=pl.BlockSpec((rows, cols), lambda k: (0, 0)),
        out_shape=jax.ShapeDtypeStruct((rows, cols), jnp.float32),
        scratch_shapes=[
            pltpu.VMEM((CHUNK // LANES, LANES), jnp.int32),
            pltpu.VMEM((2 * rows, 2 * cols), jnp.float32),
        ],
        name="gathered",
    )(vir_irrep.reshape(1, nv), occ_irrep.reshape(1, no), v, t)


def reduced(first, second):
    to_first, to_second = [], []
    for z in range(4):
        b = z // 2
        to_first += [(b * 4 + z, (1 - b) * 4 + (z ^ 1)), ((1 - b) * 4 + z, (1 - b) * 4 + (z ^ 3))]
        to_second += [(b * 4 + z, (1 - b) * 4 + z), ((1 - b) * 4 + z, (1 - b) * 4 + (z ^ 2))]
    got = lax.ppermute(first, ("vir", "rep"), to_first) + lax.ppermute(second, ("vir", "rep"), to_second)
    width = got.shape[1] // 2
    return got[:, :width] + lax.ppermute(got[:, width:], "vir", [(0, 1), (1, 0)])


def per_device(integrals, amplitudes, vir_irrep, occ_irrep):
    rows, depth = integrals.shape
    cols = amplitudes.shape[1]
    if lax.axis_size("vir") != 2 or lax.axis_size("rep") != 4 or cols != LANES or rows % 16:
        piece = lax.all_gather(amplitudes, "vir", axis=1, tiled=True)
        partial = gathered_product(integrals, piece, vir_irrep, occ_irrep)
        return lax.psum_scatter(partial, "rep", scatter_dimension=1, tiled=True)

    other = lax.ppermute(integrals, "vir", [(0, 1), (1, 0)])
    part, high, low, g_ef, *rest = own_product(integrals, amplitudes, vir_irrep)
    tails = []
    if rest:
        t, part = lax.optimization_barrier((amplitudes, part))
        tails = tails_of(rest[0], t)
    first, second = messages(other, tails, part, high, low, g_ef, vir_irrep, occ_irrep)
    return reduced(first, second)


def solution(mesh):
    return jax.shard_map(
        per_device,
        mesh=mesh,
        in_specs=(P("vir", "rep"), P("rep", ("occ", "vir")), P(), P()),
        out_specs=P("vir", ("occ", "rep")),
        check_vma=False,
    )
```

```python
import jax
import jax.numpy as jnp
from jax import lax
from jax.experimental import pallas as pl
from jax.experimental.pallas import tpu as pltpu
from jax.sharding import PartitionSpec as P

LANES = 128
SUB = 256
CHUNK = 8192
BLOCK = 2048
GROUP = 16


def lookup(table_ref, ids):
    found = None
    low = jnp.bitwise_and(ids, LANES - 1)
    for part in range(table_ref.shape[1] // LANES):
        row = jnp.broadcast_to(table_ref[:, part * LANES:(part + 1) * LANES], ids.shape)
        here = jnp.take_along_axis(row, low, axis=1, mode="promise_in_bounds")
        found = here if found is None else jnp.where(ids >= part * LANES, here, found)
    return found


def pair_labels(table_ref, width, ids):
    first = lax.div(ids, jnp.int32(width))
    return jnp.bitwise_xor(lookup(table_ref, first), lookup(table_ref, ids - first * width))


def halves(x):
    high = x.astype(jnp.bfloat16)
    return high, (x - high.astype(jnp.float32)).astype(jnp.bfloat16)


def up(size, unit):
    return pl.cdiv(size, unit) * unit


def iota(shape, axis):
    return lax.broadcasted_iota(jnp.int32, shape, axis)


def joined(parts):
    return parts[0] if len(parts) == 1 else jnp.concatenate(parts, axis=1)


def kept_columns(total, labels, otab, no, col0):
    parts = []
    for j in range(total.shape[1] // LANES):
        g_ij = pair_labels(otab, no, col0 + j * LANES + iota((8, LANES), 1))[0:1, :]
        parts.append(jnp.where(labels == g_ij, total[:, j * LANES:(j + 1) * LANES], 0.0))
    return joined(parts)


def padded_table(scratch, table_ref):
    scratch[:, :table_ref.shape[1]] = table_ref[...]


def folded(both, rows, cols):
    return (both[:rows, :cols] + (both[:rows, cols:] + both[rows:, :cols])) + both[rows:, cols:]


def chunks_of(depth):
    return [(at, min(CHUNK, depth - at)) for at in range(0, depth, CHUNK)]


def masked_rows(v_ref, first, g_ref, labels, at, size):
    high, low = [], []
    for j in range(at // LANES, (at + size) // LANES):
        keep = labels == g_ref[j:j + 1, :]
        h, l = halves(jnp.where(keep, v_ref[:, j * LANES - first:(j + 1) * LANES - first], 0.0))
        high.append(h)
        low.append(l)
    return jnp.concatenate([joined(high), joined(low)], axis=0)


def tails_of(v, t):
    base = t.shape[0] // LANES * LANES
    fill = LANES - (t.shape[0] - base)
    return [v, jnp.pad(t[base:], ((0, fill), (0, 0)))]


def own_product(v, t, vir_irrep):
    rows, depth = v.shape
    cols = t.shape[1]
    nv = vir_irrep.shape[0]
    base = depth // LANES * LANES
    tiles = up(pl.cdiv(depth, LANES), 8)
    parts = chunks_of(base)
    tail = int(depth > base)

    def kernel(vir_ref, v_hbm, t_hbm, *refs):
        part_ref, high_ref, low_ref, g_ref = refs[:4]
        raw, vtab, vbuf, tbuf, rsem, vsem, tsem = refs[-7:]
        labels_in = pltpu.make_async_copy(vir_ref, raw, rsem)
        labels_in.start()
        rows_in = [pltpu.make_async_copy(v_hbm.at[pl.ds(i * GROUP, GROUP), :], vbuf.at[pl.ds(i * GROUP, GROUP), :], vsem.at[i])
                   for i in range(rows // GROUP)]
        parts_in = [pltpu.make_async_copy(t_hbm.at[pl.ds(at, size), :], tbuf.at[pl.ds(at, size), :], tsem.at[c])
                    for c, (at, size) in enumerate(parts)]
        for copy in rows_in + parts_in:
            copy.start()
        labels_in.wait()
        padded_table(vtab, raw)
        local = iota((tiles, LANES), 0) * LANES + iota((tiles, LANES), 1)
        g_ef = pair_labels(vtab, nv, lax.axis_index("rep") * depth + local)
        g_ref[...] = jnp.where(local < depth, g_ef, -1)
        labels = pair_labels(vtab, nv, lax.axis_index("vir") * rows + iota((rows, LANES), 0))
        for copy in rows_in:
            copy.wait()
        if depth > base:
            rest = refs[4]
            rest[...] = jnp.zeros_like(rest)
            rest[:, :depth - base] = vbuf[:, base:]
        total = None
        for c, (at, size) in enumerate(parts):
            parts_in[c].wait()
            for s in range(at, at + size, SUB):
                end = min(s + SUB, at + size)
                high, low = halves(tbuf[s:end, :])
                high_ref[s:end, :] = high
                low_ref[s:end, :] = low
                got = jnp.dot(masked_rows(vbuf, 0, g_ref, labels, s, end - s), jnp.concatenate([high, low], axis=1),
                              preferred_element_type=jnp.float32)
                total = got if total is None else total + got
        part_ref[...] = folded(total, rows, cols)

    vmem = pl.BlockSpec(memory_space=pltpu.VMEM)
    hbm = pl.BlockSpec(memory_space=pltpu.HBM)
    return pl.pallas_call(
        kernel,
        in_specs=[hbm, hbm, hbm],
        out_specs=[vmem] * (4 + tail),
        out_shape=[
            pltpu.VMEM((rows, cols), jnp.float32),
            pltpu.VMEM((base, cols), jnp.bfloat16),
            pltpu.VMEM((base, cols), jnp.bfloat16),
            pltpu.VMEM((tiles, LANES), jnp.int32),
        ] + [pltpu.VMEM((rows, LANES), jnp.float32)] * tail,
        scratch_shapes=[
            pltpu.VMEM((1, nv), jnp.int32),
            pltpu.VMEM((1, up(nv, LANES)), jnp.int32),
            pltpu.VMEM((rows, depth), jnp.float32),
            pltpu.VMEM((base, cols), jnp.float32),
            pltpu.SemaphoreType.DMA(()),
            pltpu.SemaphoreType.DMA((rows // GROUP,)),
            pltpu.SemaphoreType.DMA((len(parts),)),
        ],
        compiler_params=pltpu.CompilerParams(vmem_limit_bytes=32 << 20),
        name="own",
    )(*(pltpu.with_memory_space_constraint(x, pltpu.HBM) for x in (vir_irrep.reshape(1, nv), v, t)))


def messages(v, tails, part, high, low, g_ef, vir_irrep, occ_irrep):
    rows, depth = v.shape
    cols = high.shape[1]
    width = cols // 2
    nv, no = vir_irrep.shape[0], occ_irrep.shape[0]
    base = depth // LANES * LANES

    def kernel(vir_ref, occ_ref, v_ref, *refs):
        tail_refs = refs[:len(tails)]
        part_ref, high_ref, low_ref, g_ref, out0, out1, vtab, otab, rest = refs[len(tails):]
        vir, rep, occ = lax.axis_index("vir"), lax.axis_index("rep"), lax.axis_index("occ")
        padded_table(vtab, vir_ref)
        padded_table(otab, occ_ref)
        mine = pair_labels(vtab, nv, vir * rows + iota((rows, LANES), 0))
        theirs = pair_labels(vtab, nv, (1 - vir) * rows + iota((rows, LANES), 0))
        total = None
        own = part_ref[...]
        if tails:
            v_tail, t_tail = tail_refs
            both = jnp.concatenate(halves(t_tail[...]), axis=1)
            rest[...] = jnp.zeros_like(rest)
            rest[:, :depth - base] = v_ref[:, base:]
            total = jnp.dot(masked_rows(rest, base, g_ref, theirs, base, LANES), both, preferred_element_type=jnp.float32)
            more = jnp.dot(masked_rows(v_tail, base, g_ref, mine, base, LANES), both, preferred_element_type=jnp.float32)
            own = own + folded(more, rows, cols)
        for s in range(0, base, SUB):
            end = min(s + SUB, base)
            both = jnp.concatenate([high_ref[s:end, :], low_ref[s:end, :]], axis=1)
            got = jnp.dot(masked_rows(v_ref, 0, g_ref, theirs, s, end - s), both, preferred_element_type=jnp.float32)
            total = got if total is None else total + got
        col0 = (occ * 2 + vir) * cols
        own = kept_columns(own, mine, otab, no, col0)
        other = kept_columns(folded(total, rows, cols), theirs, otab, no, col0)
        same = vir == lax.div(rep, 2)
        first = jnp.where(same, other, own)
        second = jnp.where(same, own, other)
        upper = lax.rem(rep, 2) == 0
        first_turned = pltpu.roll(first, width, 1)
        second_turned = pltpu.roll(second, width, 1)
        left = iota((rows, cols), 1) < width
        out0[...] = jnp.where(left, jnp.where(upper, first_turned, first), jnp.where(upper, second, second_turned))
        out1[...] = jnp.where(left, jnp.where(upper, first, first_turned), jnp.where(upper, second_turned, second))

    vmem = pl.BlockSpec(memory_space=pltpu.VMEM)
    return pl.pallas_call(
        kernel,
        in_specs=[vmem] * (7 + len(tails)),
        out_specs=[vmem] * 2,
        out_shape=[jax.ShapeDtypeStruct((rows, cols), jnp.float32)] * 2,
        scratch_shapes=[
            pltpu.VMEM((1, up(nv, LANES)), jnp.int32),
            pltpu.VMEM((1, up(no, LANES)), jnp.int32),
            pltpu.VMEM((rows, LANES), jnp.float32),
        ],
        compiler_params=pltpu.CompilerParams(vmem_limit_bytes=32 << 20),
        name="messages",
    )(vir_irrep.reshape(1, nv), occ_irrep.reshape(1, no), v, *tails, part, high, low, g_ef)


def gathered_product(v, t, vir_irrep, occ_irrep):
    rows, depth = v.shape
    cols = t.shape[1]
    nv, no = vir_irrep.shape[0], occ_irrep.shape[0]
    steps = pl.cdiv(depth, BLOCK)

    def kernel(vtab, otab, v_ref, t_ref, out_ref, g_ref, acc):
        step = pl.program_id(0)
        labels = pair_labels(vtab, nv, lax.axis_index("vir") * rows + iota((rows, LANES), 0))
        shape = (BLOCK // LANES, LANES)
        local = step * BLOCK + iota(shape, 0) * LANES + iota(shape, 1)
        g_ef = pair_labels(vtab, nv, lax.axis_index("rep") * depth + local)
        g_ref[...] = jnp.where(local < depth, g_ef, -1)
        total = None
        for s in range(0, BLOCK, SUB):
            block = jnp.where(step * BLOCK + s + iota((SUB, cols), 0) < depth, t_ref[s:s + SUB, :], 0.0)
            both = jnp.concatenate(halves(block), axis=1)
            got = jnp.dot(masked_rows(v_ref, 0, g_ref, labels, s, SUB), both, preferred_element_type=jnp.float32)
            total = got if total is None else total + got
        acc[...] = jnp.where(step == 0, total, acc[...] + total)

        @pl.when(step == steps - 1)
        def _():
            out_ref[...] = kept_columns(folded(acc[...], rows, cols), labels, otab, no, lax.axis_index("occ") * cols)

    return pl.pallas_call(
        kernel,
        grid=(steps,),
        in_specs=[
            pl.BlockSpec((1, up(nv, LANES)), lambda k: (0, 0)),
            pl.BlockSpec((1, up(no, LANES)), lambda k: (0, 0)),
            pl.BlockSpec((rows, BLOCK), lambda k: (0, k)),
            pl.BlockSpec((BLOCK, cols), lambda k: (k, 0)),
        ],
        out_specs=pl.BlockSpec((rows, cols), lambda k: (0, 0)),
        out_shape=jax.ShapeDtypeStruct((rows, cols), jnp.float32),
        scratch_shapes=[
            pltpu.VMEM((BLOCK // LANES, LANES), jnp.int32),
            pltpu.VMEM((2 * rows, 2 * cols), jnp.float32),
        ],
        name="gathered",
    )(vir_irrep.reshape(1, nv), occ_irrep.reshape(1, no), v, t)


def reduced(first, second):
    to_first, to_second = [], []
    for z in range(4):
        b = z // 2
        to_first += [(b * 4 + z, (1 - b) * 4 + (z ^ 1)), ((1 - b) * 4 + z, (1 - b) * 4 + (z ^ 3))]
        to_second += [(b * 4 + z, (1 - b) * 4 + z), ((1 - b) * 4 + z, (1 - b) * 4 + (z ^ 2))]
    got = lax.ppermute(second, ("vir", "rep"), to_second) + lax.ppermute(first, ("vir", "rep"), to_first)
    width = got.shape[1] // 2
    return got[:, :width] + lax.ppermute(got[:, width:], "vir", [(0, 1), (1, 0)])


def per_device(integrals, amplitudes, vir_irrep, occ_irrep):
    rows, depth = integrals.shape
    cols = amplitudes.shape[1]
    if lax.axis_size("vir") != 2 or lax.axis_size("rep") != 4 or cols != LANES or rows % 16:
        piece = lax.all_gather(amplitudes, "vir", axis=1, tiled=True)
        partial = gathered_product(integrals, piece, vir_irrep, occ_irrep)
        return lax.psum_scatter(partial, "rep", scatter_dimension=1, tiled=True)

    other = lax.ppermute(integrals, "vir", [(0, 1), (1, 0)])
    part, high, low, g_ef, *rest = own_product(integrals, amplitudes, vir_irrep)
    tails = []
    if rest:
        t, part = lax.optimization_barrier((amplitudes, part))
        tails = tails_of(rest[0], t)
    first, second = messages(other, tails, part, high, low, g_ef, vir_irrep, occ_irrep)
    return reduced(first, second)


def solution(mesh):
    return jax.shard_map(
        per_device,
        mesh=mesh,
        in_specs=(P("vir", "rep"), P("rep", ("occ", "vir")), P(), P()),
        out_specs=P("vir", ("occ", "rep")),
        check_vma=False,
    )
```

```python
import jax
import jax.numpy as jnp
from jax import lax
from jax.experimental import pallas as pl
from jax.experimental.pallas import tpu as pltpu
from jax.sharding import PartitionSpec as P

LANES = 128
SUB = 256
CHUNK = 8192
BLOCK = 2048
GROUP = 16


def lookup(table_ref, ids):
    found = None
    low = jnp.bitwise_and(ids, LANES - 1)
    for part in range(table_ref.shape[1] // LANES):
        row = jnp.broadcast_to(table_ref[:, part * LANES:(part + 1) * LANES], ids.shape)
        here = jnp.take_along_axis(row, low, axis=1, mode="promise_in_bounds")
        found = here if found is None else jnp.where(ids >= part * LANES, here, found)
    return found


def pair_labels(table_ref, width, ids):
    first = lax.div(ids, jnp.int32(width))
    return jnp.bitwise_xor(lookup(table_ref, first), lookup(table_ref, ids - first * width))


def halves(x):
    high = x.astype(jnp.bfloat16)
    return high, (x - high.astype(jnp.float32)).astype(jnp.bfloat16)


def up(size, unit):
    return pl.cdiv(size, unit) * unit


def iota(shape, axis):
    return lax.broadcasted_iota(jnp.int32, shape, axis)


def joined(parts):
    return parts[0] if len(parts) == 1 else jnp.concatenate(parts, axis=1)


def kept_columns(total, labels, otab, no, col0):
    parts = []
    for j in range(total.shape[1] // LANES):
        g_ij = pair_labels(otab, no, col0 + j * LANES + iota((8, LANES), 1))[0:1, :]
        parts.append(jnp.where(labels == g_ij, total[:, j * LANES:(j + 1) * LANES], 0.0))
    return joined(parts)


def padded_table(scratch, table_ref):
    scratch[:, :table_ref.shape[1]] = table_ref[...]


def folded(both, rows, cols):
    return (both[:rows, :cols] + (both[:rows, cols:] + both[rows:, :cols])) + both[rows:, cols:]


def chunks_of(depth):
    return [(at, min(CHUNK, depth - at)) for at in range(0, depth, CHUNK)]


def masked_rows(v_ref, first, g_ref, labels, at, size):
    high, low = [], []
    for j in range(at // LANES, (at + size) // LANES):
        keep = labels == g_ref[j:j + 1, :]
        h, l = halves(jnp.where(keep, v_ref[:, j * LANES - first:(j + 1) * LANES - first], 0.0))
        high.append(h)
        low.append(l)
    return jnp.concatenate([joined(high), joined(low)], axis=0)


def tails_of(v, t):
    base = t.shape[0] // LANES * LANES
    fill = LANES - (t.shape[0] - base)
    return [v, jnp.pad(t[base:], ((0, fill), (0, 0)))]


def own_product(v, t, vir_irrep):
    rows, depth = v.shape
    cols = t.shape[1]
    nv = vir_irrep.shape[0]
    base = depth // LANES * LANES
    tiles = up(pl.cdiv(depth, LANES), 8)
    parts = chunks_of(base)
    tail = int(depth > base)

    def kernel(vir_ref, v_hbm, t_hbm, *refs):
        part_ref, high_ref, low_ref, g_ref = refs[:4]
        raw, vtab, vbuf, tbuf, rsem, vsem, tsem = refs[-7:]
        labels_in = pltpu.make_async_copy(vir_ref, raw, rsem)
        labels_in.start()
        rows_in = [pltpu.make_async_copy(v_hbm.at[pl.ds(i * GROUP, GROUP), :], vbuf.at[pl.ds(i * GROUP, GROUP), :], vsem.at[i])
                   for i in range(rows // GROUP)]
        parts_in = [pltpu.make_async_copy(t_hbm.at[pl.ds(at, size), :], tbuf.at[pl.ds(at, size), :], tsem.at[c])
                    for c, (at, size) in enumerate(parts)]
        for copy in rows_in + parts_in:
            copy.start()
        labels_in.wait()
        padded_table(vtab, raw)
        local = iota((tiles, LANES), 0) * LANES + iota((tiles, LANES), 1)
        g_ef = pair_labels(vtab, nv, lax.axis_index("rep") * depth + local)
        g_ref[...] = jnp.where(local < depth, g_ef, -1)
        labels = pair_labels(vtab, nv, lax.axis_index("vir") * rows + iota((rows, LANES), 0))
        for copy in rows_in:
            copy.wait()
        if depth > base:
            rest = refs[4]
            rest[...] = jnp.zeros_like(rest)
            rest[:, :depth - base] = vbuf[:, base:]
        total = None
        for c, (at, size) in enumerate(parts):
            parts_in[c].wait()
            for s in range(at, at + size, SUB):
                end = min(s + SUB, at + size)
                high, low = halves(tbuf[s:end, :])
                high_ref[s:end, :] = high
                low_ref[s:end, :] = low
                got = jnp.dot(masked_rows(vbuf, 0, g_ref, labels, s, end - s), jnp.concatenate([high, low], axis=1),
                              preferred_element_type=jnp.float32)
                total = got if total is None else total + got
        part_ref[...] = folded(total, rows, cols)

    vmem = pl.BlockSpec(memory_space=pltpu.VMEM)
    hbm = pl.BlockSpec(memory_space=pltpu.HBM)
    return pl.pallas_call(
        kernel,
        in_specs=[hbm, hbm, hbm],
        out_specs=[vmem] * (4 + tail),
        out_shape=[
            pltpu.VMEM((rows, cols), jnp.float32),
            pltpu.VMEM((base, cols), jnp.bfloat16),
            pltpu.VMEM((base, cols), jnp.bfloat16),
            pltpu.VMEM((tiles, LANES), jnp.int32),
        ] + [pltpu.VMEM((rows, LANES), jnp.float32)] * tail,
        scratch_shapes=[
            pltpu.VMEM((1, nv), jnp.int32),
            pltpu.VMEM((1, up(nv, LANES)), jnp.int32),
            pltpu.VMEM((rows, depth), jnp.float32),
            pltpu.VMEM((base, cols), jnp.float32),
            pltpu.SemaphoreType.DMA(()),
            pltpu.SemaphoreType.DMA((rows // GROUP,)),
            pltpu.SemaphoreType.DMA((len(parts),)),
        ],
        compiler_params=pltpu.CompilerParams(vmem_limit_bytes=32 << 20),
        name="own",
    )(*(pltpu.with_memory_space_constraint(x, pltpu.HBM) for x in (vir_irrep.reshape(1, nv), v, t)))


def messages(v, tails, part, high, low, g_ef, vir_irrep, occ_irrep):
    rows, depth = v.shape
    cols = high.shape[1]
    width = cols // 2
    nv, no = vir_irrep.shape[0], occ_irrep.shape[0]
    base = depth // LANES * LANES

    def kernel(vir_ref, occ_ref, v_ref, *refs):
        tail_refs = refs[:len(tails)]
        part_ref, high_ref, low_ref, g_ref, out0, out1, vtab, otab, rest = refs[len(tails):]
        vir, rep, occ = lax.axis_index("vir"), lax.axis_index("rep"), lax.axis_index("occ")
        padded_table(vtab, vir_ref)
        padded_table(otab, occ_ref)
        mine = pair_labels(vtab, nv, vir * rows + iota((rows, LANES), 0))
        theirs = pair_labels(vtab, nv, (1 - vir) * rows + iota((rows, LANES), 0))
        total = None
        own = part_ref[...]
        if tails:
            v_tail, t_tail = tail_refs
            both = jnp.concatenate(halves(t_tail[...]), axis=1)
            rest[...] = jnp.zeros_like(rest)
            rest[:, :depth - base] = v_ref[:, base:]
            total = jnp.dot(masked_rows(rest, base, g_ref, theirs, base, LANES), both, preferred_element_type=jnp.float32)
            more = jnp.dot(masked_rows(v_tail, base, g_ref, mine, base, LANES), both, preferred_element_type=jnp.float32)
            own = own + folded(more, rows, cols)
        for s in range(0, base, SUB):
            end = min(s + SUB, base)
            both = jnp.concatenate([high_ref[s:end, :], low_ref[s:end, :]], axis=1)
            got = jnp.dot(masked_rows(v_ref, 0, g_ref, theirs, s, end - s), both, preferred_element_type=jnp.float32)
            total = got if total is None else total + got
        col0 = (occ * 2 + vir) * cols
        own = kept_columns(own, mine, otab, no, col0)
        other = kept_columns(folded(total, rows, cols), theirs, otab, no, col0)
        same = vir == lax.div(rep, 2)
        first = jnp.where(same, other, own)
        second = jnp.where(same, own, other)
        upper = lax.rem(rep, 2) == 0
        first_turned = pltpu.roll(first, width, 1)
        second_turned = pltpu.roll(second, width, 1)
        left = iota((rows, cols), 1) < width
        out0[...] = jnp.where(left, jnp.where(upper, first_turned, first), jnp.where(upper, second, second_turned))
        out1[...] = jnp.where(left, jnp.where(upper, first, first_turned), jnp.where(upper, second_turned, second))

    vmem = pl.BlockSpec(memory_space=pltpu.VMEM)
    return pl.pallas_call(
        kernel,
        in_specs=[vmem] * (7 + len(tails)),
        out_specs=[vmem] * 2,
        out_shape=[jax.ShapeDtypeStruct((rows, cols), jnp.float32)] * 2,
        scratch_shapes=[
            pltpu.VMEM((1, up(nv, LANES)), jnp.int32),
            pltpu.VMEM((1, up(no, LANES)), jnp.int32),
            pltpu.VMEM((rows, LANES), jnp.float32),
        ],
        compiler_params=pltpu.CompilerParams(vmem_limit_bytes=32 << 20),
        name="messages",
    )(vir_irrep.reshape(1, nv), occ_irrep.reshape(1, no), v, *tails, part, high, low, g_ef)


def gathered_product(v, t, vir_irrep, occ_irrep):
    rows, depth = v.shape
    cols = t.shape[1]
    nv, no = vir_irrep.shape[0], occ_irrep.shape[0]
    steps = pl.cdiv(depth, BLOCK)

    def kernel(vtab, otab, v_ref, t_ref, out_ref, g_ref, acc):
        step = pl.program_id(0)
        labels = pair_labels(vtab, nv, lax.axis_index("vir") * rows + iota((rows, LANES), 0))
        shape = (BLOCK // LANES, LANES)
        local = step * BLOCK + iota(shape, 0) * LANES + iota(shape, 1)
        g_ef = pair_labels(vtab, nv, lax.axis_index("rep") * depth + local)
        g_ref[...] = jnp.where(local < depth, g_ef, -1)
        total = None
        for s in range(0, BLOCK, SUB):
            block = jnp.where(step * BLOCK + s + iota((SUB, cols), 0) < depth, t_ref[s:s + SUB, :], 0.0)
            both = jnp.concatenate(halves(block), axis=1)
            got = jnp.dot(masked_rows(v_ref, 0, g_ref, labels, s, SUB), both, preferred_element_type=jnp.float32)
            total = got if total is None else total + got
        acc[...] = jnp.where(step == 0, total, acc[...] + total)

        @pl.when(step == steps - 1)
        def _():
            out_ref[...] = kept_columns(folded(acc[...], rows, cols), labels, otab, no, lax.axis_index("occ") * cols)

    return pl.pallas_call(
        kernel,
        grid=(steps,),
        in_specs=[
            pl.BlockSpec((1, up(nv, LANES)), lambda k: (0, 0)),
            pl.BlockSpec((1, up(no, LANES)), lambda k: (0, 0)),
            pl.BlockSpec((rows, BLOCK), lambda k: (0, k)),
            pl.BlockSpec((BLOCK, cols), lambda k: (k, 0)),
        ],
        out_specs=pl.BlockSpec((rows, cols), lambda k: (0, 0)),
        out_shape=jax.ShapeDtypeStruct((rows, cols), jnp.float32),
        scratch_shapes=[
            pltpu.VMEM((BLOCK // LANES, LANES), jnp.int32),
            pltpu.VMEM((2 * rows, 2 * cols), jnp.float32),
        ],
        name="gathered",
    )(vir_irrep.reshape(1, nv), occ_irrep.reshape(1, no), v, t)


def reduced(first, second):
    to_first, to_second = [], []
    for z in range(4):
        b = z // 2
        to_first += [(b * 4 + z, (1 - b) * 4 + (z ^ 1)), ((1 - b) * 4 + z, (1 - b) * 4 + (z ^ 3))]
        to_second += [(b * 4 + z, (1 - b) * 4 + z), ((1 - b) * 4 + z, (1 - b) * 4 + (z ^ 2))]
    got = lax.ppermute(second, ("vir", "rep"), to_second) + lax.ppermute(first, ("vir", "rep"), to_first)
    width = got.shape[1] // 2
    return got[:, :width] + lax.ppermute(got, "vir", [(0, 1), (1, 0)])[:, width:]


def per_device(integrals, amplitudes, vir_irrep, occ_irrep):
    rows, depth = integrals.shape
    cols = amplitudes.shape[1]
    if lax.axis_size("vir") != 2 or lax.axis_size("rep") != 4 or cols != LANES or rows % 16:
        piece = lax.all_gather(amplitudes, "vir", axis=1, tiled=True)
        partial = gathered_product(integrals, piece, vir_irrep, occ_irrep)
        return lax.psum_scatter(partial, "rep", scatter_dimension=1, tiled=True)

    other = lax.ppermute(integrals, "vir", [(0, 1), (1, 0)])
    part, high, low, g_ef, *rest = own_product(integrals, amplitudes, vir_irrep)
    tails = []
    if rest:
        t, part = lax.optimization_barrier((amplitudes, part))
        tails = tails_of(rest[0], t)
    first, second = messages(other, tails, part, high, low, g_ef, vir_irrep, occ_irrep)
    return reduced(first, second)


def solution(mesh):
    return jax.shard_map(
        per_device,
        mesh=mesh,
        in_specs=(P("vir", "rep"), P("rep", ("occ", "vir")), P(), P()),
        out_specs=P("vir", ("occ", "rep")),
        check_vma=False,
    )
```

```python
import jax
import jax.numpy as jnp
from jax import lax
from jax.experimental import pallas as pl
from jax.experimental.pallas import tpu as pltpu
from jax.sharding import PartitionSpec as P

LANES = 128
SUB = 256
CHUNK = 8192
BLOCK = 2048
GROUP = 16


def lookup(table_ref, ids):
    found = None
    low = jnp.bitwise_and(ids, LANES - 1)
    for part in range(table_ref.shape[1] // LANES):
        row = jnp.broadcast_to(table_ref[:, part * LANES:(part + 1) * LANES], ids.shape)
        here = jnp.take_along_axis(row, low, axis=1, mode="promise_in_bounds")
        found = here if found is None else jnp.where(ids >= part * LANES, here, found)
    return found


def pair_labels(table_ref, width, ids):
    first = lax.div(ids, jnp.int32(width))
    return jnp.bitwise_xor(lookup(table_ref, first), lookup(table_ref, ids - first * width))


def halves(x):
    high = x.astype(jnp.bfloat16)
    return high, (x - high.astype(jnp.float32)).astype(jnp.bfloat16)


def up(size, unit):
    return pl.cdiv(size, unit) * unit


def iota(shape, axis):
    return lax.broadcasted_iota(jnp.int32, shape, axis)


def joined(parts):
    return parts[0] if len(parts) == 1 else jnp.concatenate(parts, axis=1)


def kept_columns(total, labels, otab, no, col0):
    parts = []
    for j in range(total.shape[1] // LANES):
        g_ij = pair_labels(otab, no, col0 + j * LANES + iota((8, LANES), 1))[0:1, :]
        parts.append(jnp.where(labels == g_ij, total[:, j * LANES:(j + 1) * LANES], 0.0))
    return joined(parts)


def padded_table(scratch, table_ref):
    scratch[:, :table_ref.shape[1]] = table_ref[...]


def folded(both, rows, cols):
    return (both[:rows, :cols] + (both[:rows, cols:] + both[rows:, :cols])) + both[rows:, cols:]


def chunks_of(depth):
    return [(at, min(CHUNK, depth - at)) for at in range(0, depth, CHUNK)]


def masked_rows(v_ref, first, g_ref, labels, at, size):
    high, low = [], []
    for j in range(at // LANES, (at + size) // LANES):
        keep = labels == g_ref[j:j + 1, :]
        h, l = halves(jnp.where(keep, v_ref[:, j * LANES - first:(j + 1) * LANES - first], 0.0))
        high.append(h)
        low.append(l)
    return jnp.concatenate([joined(high), joined(low)], axis=0)


def tails_of(v, t):
    base = t.shape[0] // LANES * LANES
    fill = LANES - (t.shape[0] - base)
    return [v, jnp.pad(t[base:], ((0, fill), (0, 0)))]


def own_product(v, t, vir_irrep):
    rows, depth = v.shape
    cols = t.shape[1]
    nv = vir_irrep.shape[0]
    base = depth // LANES * LANES
    tiles = up(pl.cdiv(depth, LANES), 8)
    parts = chunks_of(base)
    tail = int(depth > base)

    def kernel(vir_ref, v_hbm, t_hbm, *refs):
        part_ref, high_ref, low_ref, g_ref, mine_ref, theirs_ref = refs[:6]
        raw, vtab, vbuf, tbuf, rsem, vsem, tsem = refs[-7:]
        labels_in = pltpu.make_async_copy(vir_ref, raw, rsem)
        labels_in.start()
        rows_in = [pltpu.make_async_copy(v_hbm.at[pl.ds(i * GROUP, GROUP), :], vbuf.at[pl.ds(i * GROUP, GROUP), :], vsem.at[i])
                   for i in range(rows // GROUP)]
        parts_in = [pltpu.make_async_copy(t_hbm.at[pl.ds(at, size), :], tbuf.at[pl.ds(at, size), :], tsem.at[c])
                    for c, (at, size) in enumerate(parts)]
        for copy in rows_in + parts_in:
            copy.start()
        labels_in.wait()
        padded_table(vtab, raw)
        local = iota((tiles, LANES), 0) * LANES + iota((tiles, LANES), 1)
        g_ef = pair_labels(vtab, nv, lax.axis_index("rep") * depth + local)
        g_ref[...] = jnp.where(local < depth, g_ef, -1)
        vir = lax.axis_index("vir")
        labels = pair_labels(vtab, nv, vir * rows + iota((rows, LANES), 0))
        mine_ref[...] = labels
        theirs_ref[...] = pair_labels(vtab, nv, (1 - vir) * rows + iota((rows, LANES), 0))
        for copy in rows_in:
            copy.wait()
        if depth > base:
            rest = refs[6]
            rest[...] = jnp.zeros_like(rest)
            rest[:, :depth - base] = vbuf[:, base:]
        total = None
        for c, (at, size) in enumerate(parts):
            parts_in[c].wait()
            for s in range(at, at + size, SUB):
                end = min(s + SUB, at + size)
                high, low = halves(tbuf[s:end, :])
                high_ref[s:end, :] = high
                low_ref[s:end, :] = low
                got = jnp.dot(masked_rows(vbuf, 0, g_ref, labels, s, end - s), jnp.concatenate([high, low], axis=1),
                              preferred_element_type=jnp.float32)
                total = got if total is None else total + got
        part_ref[...] = folded(total, rows, cols)

    vmem = pl.BlockSpec(memory_space=pltpu.VMEM)
    hbm = pl.BlockSpec(memory_space=pltpu.HBM)
    return pl.pallas_call(
        kernel,
        in_specs=[hbm, hbm, hbm],
        out_specs=[vmem] * (6 + tail),
        out_shape=[
            pltpu.VMEM((rows, cols), jnp.float32),
            pltpu.VMEM((base, cols), jnp.bfloat16),
            pltpu.VMEM((base, cols), jnp.bfloat16),
            pltpu.VMEM((tiles, LANES), jnp.int32),
            pltpu.VMEM((rows, LANES), jnp.int32),
            pltpu.VMEM((rows, LANES), jnp.int32),
        ] + [pltpu.VMEM((rows, LANES), jnp.float32)] * tail,
        scratch_shapes=[
            pltpu.VMEM((1, nv), jnp.int32),
            pltpu.VMEM((1, up(nv, LANES)), jnp.int32),
            pltpu.VMEM((rows, depth), jnp.float32),
            pltpu.VMEM((base, cols), jnp.float32),
            pltpu.SemaphoreType.DMA(()),
            pltpu.SemaphoreType.DMA((rows // GROUP,)),
            pltpu.SemaphoreType.DMA((len(parts),)),
        ],
        compiler_params=pltpu.CompilerParams(vmem_limit_bytes=32 << 20),
        name="own",
    )(*(pltpu.with_memory_space_constraint(x, pltpu.HBM) for x in (vir_irrep.reshape(1, nv), v, t)))


def messages(v, tails, part, high, low, g_ef, g_mine, g_theirs, occ_irrep):
    rows, depth = v.shape
    cols = high.shape[1]
    width = cols // 2
    no = occ_irrep.shape[0]
    base = depth // LANES * LANES

    def kernel(occ_ref, v_ref, *refs):
        tail_refs = refs[:len(tails)]
        part_ref, high_ref, low_ref, g_ref, mine_ref, theirs_ref, out0, out1, otab, rest = refs[len(tails):]
        vir, rep, occ = lax.axis_index("vir"), lax.axis_index("rep"), lax.axis_index("occ")
        padded_table(otab, occ_ref)
        mine = mine_ref[...]
        theirs = theirs_ref[...]
        total = None
        own = part_ref[...]
        if tails:
            v_tail, t_tail = tail_refs
            both = jnp.concatenate(halves(t_tail[...]), axis=1)
            rest[...] = jnp.zeros_like(rest)
            rest[:, :depth - base] = v_ref[:, base:]
            total = jnp.dot(masked_rows(rest, base, g_ref, theirs, base, LANES), both, preferred_element_type=jnp.float32)
            more = jnp.dot(masked_rows(v_tail, base, g_ref, mine, base, LANES), both, preferred_element_type=jnp.float32)
            own = own + folded(more, rows, cols)
        for s in range(0, base, SUB):
            end = min(s + SUB, base)
            both = jnp.concatenate([high_ref[s:end, :], low_ref[s:end, :]], axis=1)
            got = jnp.dot(masked_rows(v_ref, 0, g_ref, theirs, s, end - s), both, preferred_element_type=jnp.float32)
            total = got if total is None else total + got
        col0 = (occ * 2 + vir) * cols
        own = kept_columns(own, mine, otab, no, col0)
        other = kept_columns(folded(total, rows, cols), theirs, otab, no, col0)
        same = vir == lax.div(rep, 2)
        first = jnp.where(same, other, own)
        second = jnp.where(same, own, other)
        upper = lax.rem(rep, 2) == 0
        first_turned = pltpu.roll(first, width, 1)
        second_turned = pltpu.roll(second, width, 1)
        left = iota((rows, cols), 1) < width
        out0[...] = jnp.where(left, jnp.where(upper, first_turned, first), jnp.where(upper, second, second_turned))
        out1[...] = jnp.where(left, jnp.where(upper, first, first_turned), jnp.where(upper, second_turned, second))

    vmem = pl.BlockSpec(memory_space=pltpu.VMEM)
    return pl.pallas_call(
        kernel,
        in_specs=[vmem] * (8 + len(tails)),
        out_specs=[vmem] * 2,
        out_shape=[jax.ShapeDtypeStruct((rows, cols), jnp.float32)] * 2,
        scratch_shapes=[
            pltpu.VMEM((1, up(no, LANES)), jnp.int32),
            pltpu.VMEM((rows, LANES), jnp.float32),
        ],
        compiler_params=pltpu.CompilerParams(vmem_limit_bytes=32 << 20),
        name="messages",
    )(occ_irrep.reshape(1, no), v, *tails, part, high, low, g_ef, g_mine, g_theirs)


def gathered_product(v, t, vir_irrep, occ_irrep):
    rows, depth = v.shape
    cols = t.shape[1]
    nv, no = vir_irrep.shape[0], occ_irrep.shape[0]
    steps = pl.cdiv(depth, BLOCK)

    def kernel(vtab, otab, v_ref, t_ref, out_ref, g_ref, acc):
        step = pl.program_id(0)
        labels = pair_labels(vtab, nv, lax.axis_index("vir") * rows + iota((rows, LANES), 0))
        shape = (BLOCK // LANES, LANES)
        local = step * BLOCK + iota(shape, 0) * LANES + iota(shape, 1)
        g_ef = pair_labels(vtab, nv, lax.axis_index("rep") * depth + local)
        g_ref[...] = jnp.where(local < depth, g_ef, -1)
        total = None
        for s in range(0, BLOCK, SUB):
            block = jnp.where(step * BLOCK + s + iota((SUB, cols), 0) < depth, t_ref[s:s + SUB, :], 0.0)
            both = jnp.concatenate(halves(block), axis=1)
            got = jnp.dot(masked_rows(v_ref, 0, g_ref, labels, s, SUB), both, preferred_element_type=jnp.float32)
            total = got if total is None else total + got
        acc[...] = jnp.where(step == 0, total, acc[...] + total)

        @pl.when(step == steps - 1)
        def _():
            out_ref[...] = kept_columns(folded(acc[...], rows, cols), labels, otab, no, lax.axis_index("occ") * cols)

    return pl.pallas_call(
        kernel,
        grid=(steps,),
        in_specs=[
            pl.BlockSpec((1, up(nv, LANES)), lambda k: (0, 0)),
            pl.BlockSpec((1, up(no, LANES)), lambda k: (0, 0)),
            pl.BlockSpec((rows, BLOCK), lambda k: (0, k)),
            pl.BlockSpec((BLOCK, cols), lambda k: (k, 0)),
        ],
        out_specs=pl.BlockSpec((rows, cols), lambda k: (0, 0)),
        out_shape=jax.ShapeDtypeStruct((rows, cols), jnp.float32),
        scratch_shapes=[
            pltpu.VMEM((BLOCK // LANES, LANES), jnp.int32),
            pltpu.VMEM((2 * rows, 2 * cols), jnp.float32),
        ],
        name="gathered",
    )(vir_irrep.reshape(1, nv), occ_irrep.reshape(1, no), v, t)


def reduced(first, second):
    to_first, to_second = [], []
    for z in range(4):
        b = z // 2
        to_first += [(b * 4 + z, (1 - b) * 4 + (z ^ 1)), ((1 - b) * 4 + z, (1 - b) * 4 + (z ^ 3))]
        to_second += [(b * 4 + z, (1 - b) * 4 + z), ((1 - b) * 4 + z, (1 - b) * 4 + (z ^ 2))]
    got = lax.ppermute(second, ("vir", "rep"), to_second) + lax.ppermute(first, ("vir", "rep"), to_first)
    width = got.shape[1] // 2
    return got[:, :width] + lax.ppermute(got[:, width:], "vir", [(0, 1), (1, 0)])


def per_device(integrals, amplitudes, vir_irrep, occ_irrep):
    rows, depth = integrals.shape
    cols = amplitudes.shape[1]
    if lax.axis_size("vir") != 2 or lax.axis_size("rep") != 4 or cols != LANES or rows % 16:
        piece = lax.all_gather(amplitudes, "vir", axis=1, tiled=True)
        partial = gathered_product(integrals, piece, vir_irrep, occ_irrep)
        return lax.psum_scatter(partial, "rep", scatter_dimension=1, tiled=True)

    other = lax.ppermute(integrals, "vir", [(0, 1), (1, 0)])
    part, high, low, g_ef, g_mine, g_theirs, *rest = own_product(integrals, amplitudes, vir_irrep)
    tails = []
    if rest:
        t, part = lax.optimization_barrier((amplitudes, part))
        tails = tails_of(rest[0], t)
    first, second = messages(other, tails, part, high, low, g_ef, g_mine, g_theirs, occ_irrep)
    return reduced(first, second)


def solution(mesh):
    return jax.shard_map(
        per_device,
        mesh=mesh,
        in_specs=(P("vir", "rep"), P("rep", ("occ", "vir")), P(), P()),
        out_specs=P("vir", ("occ", "rep")),
        check_vma=False,
    )
```
